32 devices in a mesh: gx: 2 (over y), gy: 4 (over z), gz: 4 (over x, core).
Axes of the slice: x: 2, y: 2, z: 4, core: 2. Of those that a mesh axis runs over, the one named last changes fastest.
Arguments:
- offsets: float32 [3, 8, 16, 16, 128], P(None, 'gx', 'gy', 'gz'), may hold values from 0 to 1
- burgers: float32 [3, 8, 16, 16, 128], P(None, 'gx', 'gy', 'gz'), may hold values from -6 to 6
- lines: float32 [3, 8, 16, 16, 128], P(None, 'gx', 'gy', 'gz'), may hold values from -3 to 3
- counts: int32 [8, 16, 16], P('gx', 'gy', 'gz'), may hold values from 1 to 128
- connect: int32 [2, 8, 16, 16, 128], P(None, 'gx', 'gy', 'gz'), may hold values from 0 to 8191
- node_pos: float32 [3, 2, 4, 4, 8192], P(None, 'gx', 'gy', 'gz'), may hold values from -6 to 6
- drag: float32 [2, 4, 4, 8192], P('gx', 'gy', 'gz'), may hold values from 0.5 to 4
- stress: float32 [3, 3], replicated, may hold values from -1 to 1
- shifts: int32 [2, 2, 4, 4], replicated, may hold values from 0 to 512, as said below
Outputs:
- migrated: float32 [6, 2, 4, 4, 9216], P(None, 'gx', 'gy', 'gz')
The draws below stay inside these ranges and needn't reach their ends.
Inputs may be any that keep to these rules, and one draw needn't show every extreme that they name: shifts[0] of the last domain along gx is 0 and shifts[1] of the first is 0; 512 is reached by both rows in every draw.
All inputs are finite; a program needn't handle non-finite values.
Results may differ from the reference program's by a relative error of at most 0.0003.
Values sent between devices are 32-bit elements; how exact they have to be, the bound alone decides.
A program may use at most 64 MiB of HBM per device.

```python
import math
import jax
import jax.numpy as jnp
from jax import lax

SEGS = 128
CX = 4
CY = 4
CZ = 4
NODES = 8192
MIG = 512
CAP = 9216
NX = 8
NY = 16
NZ = 16
N_GX = 2
N_GY = 4
N_GZ = 4


def draw_shifts(key, part):
    first_key, second_key = jax.random.split(jax.random.fold_in(key, 17))
    upward = jax.random.randint(first_key, (N_GX, N_GY, N_GZ), 0, MIG + 1)
    downward = jax.random.randint(second_key, (N_GX, N_GY, N_GZ), 0, MIG + 1)
    slab_index = lax.broadcasted_iota(jnp.int32, (N_GX, N_GY, N_GZ), 0)
    upward = jnp.where(slab_index == N_GX - 1, 0, upward)
    downward = jnp.where(slab_index == 0, 0, downward)
    upward = upward.at[0, 0, 0].set(MIG)
    downward = downward.at[N_GX - 1, 0, 0].set(MIG)
    return jnp.stack([upward, downward]).astype(jnp.int32)


def place_ends(array, rng, least, high):
    index_at = [jax.random.randint(jax.random.fold_in(rng, axis), (), 0, length) for axis, length in enumerate(array.shape)]
    longest = array.shape.index(max(array.shape))
    neighbour = index_at[:longest] + [(index_at[longest] + 1) % array.shape[longest]] + index_at[longest + 1:]
    return array.at[tuple(index_at)].set(least).at[tuple(neighbour)].set(high)


def shard_levels(own_key, dims, cuts, smallest, largest):
    gain = 1.0
    for axis_at, parts in cuts:
        heights = jax.random.uniform(jax.random.fold_in(jax.random.fold_in(own_key, 6), axis_at), (parts,), jnp.float32, smallest / len(cuts), largest / len(cuts))
        gain = gain * jnp.repeat(jnp.exp(heights), dims[axis_at] // parts).reshape((-1,) + (1,) * (len(dims) - 1 - axis_at))
    return gain


def noise(key, dims, width, reach, shards=(), kind=jnp.bfloat16):
    result = jax.random.normal(key, dims, jnp.float32) * width
    if len(shards) > 0:
        result = shard_levels(key, dims, shards, -0.22, 0.18) * result
    return jnp.clip(result, min=-reach, max=reach).astype(kind)


def setup_inputs(seed: int = 0) -> dict:
    arg_keys = jax.random.split(jax.random.key(seed), 10)
    offsets = jnp.clip(1.0 * jax.random.uniform(arg_keys[0], (3, NX, NY, NZ, SEGS), jnp.float32) ** shard_levels(arg_keys[0], (3, NX, NY, NZ, SEGS), ((1, 2), (2, 4), (3, 4)), -0.2, 0.2), 0.0, 1.0)
    burgers = noise(arg_keys[1], (3, NX, NY, NZ, SEGS), 1.0, 6.0, ((1, 2), (2, 4), (3, 4)), jnp.float32)
    lines = noise(arg_keys[2], (3, NX, NY, NZ, SEGS), 0.5, 3.0, ((1, 2), (2, 4), (3, 4)), jnp.float32)
    counts = place_ends(jax.random.randint(arg_keys[3], (NX, NY, NZ), 1, SEGS + 1), jax.random.fold_in(arg_keys[3], 1), 1, SEGS).astype(jnp.int32)
    connect = place_ends(jax.random.randint(arg_keys[4], (2, NX, NY, NZ, SEGS), 0, NODES), jax.random.fold_in(arg_keys[4], 1), 0, NODES - 1).astype(jnp.int32)
    node_pos = noise(arg_keys[5], (3, N_GX, N_GY, N_GZ, NODES), 1.0, 6.0, ((1, 2), (2, 4), (3, 4)), jnp.float32)
    drag = jnp.clip(jnp.exp(math.log(4.0) - 2.0794415 * jax.random.uniform(arg_keys[6], (N_GX, N_GY, N_GZ, NODES), jnp.float32) ** shard_levels(arg_keys[6], (N_GX, N_GY, N_GZ, NODES), ((0, 2), (1, 4), (2, 4)), -0.2, 0.2)), 0.5, 4.0)
    stress = jnp.clip(jax.random.uniform(arg_keys[7], (3, 3), jnp.float32, -1.0, 1.0), -1.0, 1.0)
    shifts = draw_shifts(jax.random.fold_in(arg_keys[9], 71), 0)
    return {"offsets": offsets, "burgers": burgers, "lines": lines, "counts": counts, "connect": connect, "node_pos": node_pos, "drag": drag, "stress": stress, "shifts": shifts}


SOFTEN_NEAR = 0.25
SOFTEN_FAR = 4.0
NEAR_SCALE = 0.0625
FAR_SCALE = 0.03125
TIME_STEP = 0.1
NEIGHBOURS = ((0, 0, 0), (1, 0, 0), (-1, 0, 0), (0, 1, 0), (0, -1, 0), (0, 0, 1), (0, 0, -1))

def as_index(value):
    return jnp.asarray(value).astype(jnp.int32)

def pair_term(target, source, offset):
    deltas = [target[axis_id][..., :, None] - source[axis_id][..., None, :] - float(offset[axis_id]) for axis_id in range(3)]
    radius = deltas[0] * deltas[0] + deltas[1] * deltas[1] + deltas[2] * deltas[2] + SOFTEN_NEAR
    inverse = lax.rsqrt(radius)
    burgers_dot = target[3][..., :, None] * source[3][..., None, :] + target[4][..., :, None] * source[4][..., None, :] + target[5][..., :, None] * source[5][..., None, :]
    line_dot = target[6][..., :, None] * source[6][..., None, :] + target[7][..., :, None] * source[7][..., None, :] + target[8][..., :, None] * source[8][..., None, :]
    weight = burgers_dot * line_dot * inverse * inverse * inverse
    return jnp.stack([lax.optimization_barrier(jnp.sum(weight * deltas[axis_id], axis=-1)) for axis_id in range(3)])

def far_stress(moments, centers, cells):
    distance = SOFTEN_FAR + jnp.zeros((cells.shape[1], centers.shape[1]), jnp.float32)
    for axis_id in range(3):
        gap = cells[axis_id][:, None] - centers[axis_id][None, :]
        distance = distance + gap * gap
    weights = lax.rsqrt(distance)
    return jnp.dot(moments, weights.T, precision=lax.Precision.HIGHEST, preferred_element_type=jnp.float32)

def segment_force(target, sigma):
    burgers = target[3:6]
    line = target[6:9]
    pulled = [sigma[row, 0][..., None] * burgers[0] + sigma[row, 1][..., None] * burgers[1] + sigma[row, 2][..., None] * burgers[2] for row in range(3)]
    return jnp.stack([pulled[1] * line[2] - pulled[2] * line[1], pulled[2] * line[0] - pulled[0] * line[2], pulled[0] * line[1] - pulled[1] * line[0]])

def coarse_moments(stacked):
    product = jnp.einsum('axyzk,bxyzk->abxyz', stacked[3:6], stacked[6:9], precision=lax.Precision.HIGHEST)
    sx, sy, sz = (product.shape[2], product.shape[3], product.shape[4])
    return product.reshape(9, sx // 2, 2, sy // 2, 2, sz // 2, 2).sum(axis=(2, 4, 6))

def migrate_index(up_prev, down_own, up_own, down_next, nodes, margin, capacity):
    position = lax.broadcasted_iota(jnp.int32, up_prev.shape + (capacity,), len(up_prev.shape))
    upper_in = up_prev[..., None]
    kept = (nodes - up_own - down_own)[..., None]
    source = jnp.where(position < upper_in, margin - upper_in + position, jnp.where(position < upper_in + kept, margin + down_own[..., None] + position - upper_in, margin + nodes + position - upper_in - kept))
    live = position < upper_in + kept + down_next[..., None]
    return (jnp.clip(source, 0, capacity - 1).astype(jnp.int32), live)

def reference(offsets, burgers, lines, counts, connect, node_pos, drag, stress, shifts):
    mask = (lax.broadcasted_iota(jnp.int32, (NX, NY, NZ, SEGS), 3) < counts[..., None]).astype(jnp.float32)
    stacked = jnp.concatenate([offsets, burgers * mask[None], lines], axis=0)
    padded = jnp.pad(stacked, ((0, 0), (1, 1), (1, 1), (1, 1), (0, 0)))
    moments = coarse_moments(stacked).reshape(9, -1)
    coarse_grid = (NX // 2, NY // 2, NZ // 2)
    centers = jnp.stack([(2 * lax.broadcasted_iota(jnp.int32, coarse_grid, axis_id) + 1).astype(jnp.float32).reshape(-1) for axis_id in range(3)])
    zero = as_index(0)

    def plane(index):
        index = as_index(index)
        target = lax.dynamic_slice(stacked, (zero, index, zero, zero, zero), (9, 1, NY, NZ, SEGS))
        near = jnp.zeros((3, 1, NY, NZ, SEGS), jnp.float32)
        for offset in NEIGHBOURS:
            starts = (zero, as_index(index + 1 + offset[0]), as_index(1 + offset[1]), as_index(1 + offset[2]), zero)
            source = lax.dynamic_slice(padded, starts, (9, 1, NY, NZ, SEGS))
            near = near + pair_term(target, source, offset)
        cell_x = jnp.zeros((NY, NZ), jnp.float32) + index.astype(jnp.float32) + 0.5
        cell_y = lax.broadcasted_iota(jnp.int32, (NY, NZ), 0).astype(jnp.float32) + 0.5
        cell_z = lax.broadcasted_iota(jnp.int32, (NY, NZ), 1).astype(jnp.float32) + 0.5
        cells = jnp.stack([cell_x.reshape(-1), cell_y.reshape(-1), cell_z.reshape(-1)])
        sigma = FAR_SCALE * far_stress(moments, centers, cells).reshape(3, 3, 1, NY, NZ) + stress[:, :, None, None, None]
        return NEAR_SCALE * near + segment_force(target, sigma)
    planes = lax.map(plane, jnp.arange(NX, dtype=jnp.int32))
    total = jnp.moveaxis(planes[:, :, 0], 0, 1)
    domain_x = lax.broadcasted_iota(jnp.int32, (NX, NY, NZ), 0) // CX
    domain_y = lax.broadcasted_iota(jnp.int32, (NX, NY, NZ), 1) // CY
    domain_z = lax.broadcasted_iota(jnp.int32, (NX, NY, NZ), 2) // CZ
    domain = (domain_x * N_GY + domain_y) * N_GZ + domain_z
    global_ids = (connect + (domain * NODES)[None, :, :, :, None]).astype(jnp.int32)
    halves = 0.5 * total.reshape(3, -1)
    values = jnp.concatenate([halves, halves], axis=1).T
    node_count = N_GX * N_GY * N_GZ * NODES
    node_force = jax.ops.segment_sum(values, global_ids.reshape(-1), num_segments=node_count).T
    node_force = node_force.reshape(3, N_GX, N_GY, N_GZ, NODES)
    velocity = node_force / drag[None]
    fields = jnp.concatenate([node_pos + TIME_STEP * velocity, velocity], axis=0)
    empty = jnp.zeros((6, 1, N_GY, N_GZ, MIG), jnp.float32)
    from_below = jnp.concatenate([empty, fields[:, :-1, :, :, NODES - MIG:]], axis=1)
    from_above = jnp.concatenate([fields[:, 1:, :, :, :MIG], empty], axis=1)
    sectioning = jnp.concatenate([from_below, fields, from_above], axis=4)
    zero_row = jnp.zeros((1, N_GY, N_GZ), jnp.int32)
    up_own = shifts[0]
    down_own = shifts[1]
    up_prev = jnp.concatenate([zero_row, up_own[:-1]], axis=0)
    down_next = jnp.concatenate([down_own[1:], zero_row], axis=0)
    source, live = migrate_index(up_prev, down_own, up_own, down_next, NODES, MIG, CAP)
    picked = jnp.take_along_axis(sectioning, jnp.broadcast_to(source[None], sectioning.shape), axis=4)
    return jnp.where(live[None], picked, 0.0)
```

```python
import functools

import jax
import jax.numpy as jnp
import numpy as np
from jax import lax
from jax.experimental import pallas as pl
from jax.experimental.pallas import tpu as pltpu
from jax.sharding import PartitionSpec as P

MIG = 512
SOFTEN_NEAR = 0.25
SOFTEN_FAR = 4.0
NEAR_SCALE = 0.0625
FAR_SCALE = 0.03125
TIME_STEP = 0.1
AXES = ("gx", "gy", "gz")
MESH = pl.DeviceIdType.MESH
VM = pl.BlockSpec(memory_space=pltpu.VMEM)
SM = pl.BlockSpec(memory_space=pltpu.SMEM)
LANES = 128
STEP = 16


def prep_kernel(grid, off, bur, lin, counts, code, stacked, faces_x, faces_y, faces_z, mom):
    cx, cy, cz = grid
    cells = cx * cy * cz
    live = lax.broadcasted_iota(jnp.int32, (cells, LANES), 1) < counts[...]
    for c in range(3):
        stacked[c] = off[c]
        stacked[3 + c] = jnp.where(live, bur[c], 0.0)
        stacked[6 + c] = lin[c]
    for c in range(9):
        faces_x[0, c] = stacked[c, 0 : cy * cz, :]
        faces_x[1, c] = stacked[c, cells - cy * cz : cells, :]
        for x in range(cx):
            base = x * cy * cz
            faces_y[0, c, x * cz : (x + 1) * cz, :] = stacked[c, base : base + cz, :]
            base = base + (cy - 1) * cz
            faces_y[1, c, x * cz : (x + 1) * cz, :] = stacked[c, base : base + cz, :]
        faces_z[0, c] = stacked[c, pl.ds(0, cx * cy, stride=cz), :]
        faces_z[1, c] = stacked[c, pl.ds(cz - 1, cx * cy, stride=cz), :]
    total = jnp.zeros((cells, LANES), jnp.float32)
    for a in range(3):
        for b in range(3):
            part = jnp.sum(stacked[3 + a] * stacked[6 + b], axis=1, keepdims=True)
            total = total + jnp.where(code[...] == 3 * a + b, part, 0.0)
    mom[...] = jnp.sum(total, axis=0, keepdims=True)


def exchange_kernel(sizes, fx, fy, fz, mom, hx, hy, hz, gathered, *sems):
    face_send, face_recv, mom_send, mom_recv, own_sem = sems
    index = [lax.axis_index(name) for name in AXES]
    barrier = pltpu.get_barrier_semaphore()
    peers = 0
    for name, me, n in zip(AXES, index, sizes):
        for d in range(1, n):
            pl.semaphore_signal(
                barrier, inc=1, device_id={name: lax.rem(me + d, n)}, device_id_type=MESH
            )
            peers += 1
    pl.semaphore_wait(barrier, peers)

    def moment_copies(level, src, dst):
        name, me, n = AXES[level], index[level], sizes[level]
        base = sum(size - 1 for size in sizes[:level])
        return [
            pltpu.make_async_remote_copy(
                src_ref=src,
                dst_ref=dst,
                send_sem=mom_send.at[base + d - 1],
                recv_sem=mom_recv.at[base + d - 1],
                device_id={name: lax.rem(me + d, n)},
                device_id_type=MESH,
            )
            for d in range(1, n)
        ]

    nx, ny, nz = sizes
    row = (index[0] * ny + index[1]) * nz + index[2]
    own = pltpu.make_async_copy(mom, gathered.at[pl.ds(row, 1)], own_sem)
    own.start()
    first = moment_copies(2, mom, gathered.at[pl.ds(row, 1)])
    for copy in first:
        copy.start()

    def face_copy(axis, face, halo, up):
        me, n = index[axis], sizes[axis]
        slot = 2 * axis + (0 if up else 1)
        return pltpu.make_async_remote_copy(
            src_ref=face.at[1 if up else 0],
            dst_ref=halo.at[0 if up else 1],
            send_sem=face_send.at[slot],
            recv_sem=face_recv.at[slot],
            device_id={AXES[axis]: lax.rem(me + 1, n) if up else lax.rem(me + n - 1, n)},
            device_id_type=MESH,
        )

    pairs = [(0, fx, hx), (1, fy, hy), (2, fz, hz)]

    def start_faces(axis, face, halo):
        @pl.when(index[axis] < sizes[axis] - 1)
        def _():
            face_copy(axis, face, halo, True).start()

        @pl.when(index[axis] > 0)
        def _():
            face_copy(axis, face, halo, False).start()

    for axis, face, halo in pairs:
        start_faces(axis, face, halo)
    own.wait()
    for copy in first:
        copy.wait_recv()
    block = gathered.at[pl.ds((index[0] * ny + index[1]) * nz, nz)]
    second = moment_copies(1, block, block)
    for copy in second:
        copy.start()
    for copy in second:
        copy.wait_recv()
    block = gathered.at[pl.ds(index[0] * ny * nz, ny * nz)]
    third = moment_copies(0, block, block)
    for copy in third:
        copy.start()
    for copy in third:
        copy.wait_recv()
    for axis, face, halo in pairs:

        @pl.when(index[axis] > 0)
        def _():
            face_copy(axis, face, halo, True).wait_recv()

        @pl.when(index[axis] < sizes[axis] - 1)
        def _():
            face_copy(axis, face, halo, False).wait_recv()

        @pl.when(index[axis] < sizes[axis] - 1)
        def _():
            face_copy(axis, face, halo, True).wait_send()

        @pl.when(index[axis] > 0)
        def _():
            face_copy(axis, face, halo, False).wait_send()

    for copy in first + second + third:
        copy.wait_send()


def force_kernel(
    grid, sizes, counts, where, stress, stacked, hx, hy, hz, gathered, centers, groups,
    connect, pos, drag, fields, low, high, ext, staged, rows, turned, sums, near, far, left, right, acc,
):
    cx, cy, cz = grid
    cells = cx * cy * cz
    face = (cy * cz, cx * cz, cx * cy)
    base = [cells]
    for axis in range(3):
        base.append(base[-1] + 2 * face[axis])
    ext[:, 0:cells, :] = stacked[...]
    for axis, halo in enumerate((hx, hy, hz)):
        for side in range(2):
            inside = where[axis] > 0 if side == 0 else where[axis] < sizes[axis] - 1
            start = base[axis] + side * face[axis]
            ext[:, start : start + face[axis], :] = jnp.where(inside, halo[side], 0.0)

    def far_cell(t, carry):
        x, rest = lax.div(t, cy * cz), lax.rem(t, cy * cz)
        y, z = lax.div(rest, cz), lax.rem(rest, cz)
        spot = [
            (where[axis] * grid[axis] + (x, y, z)[axis]).astype(jnp.float32) + 0.5
            for axis in range(3)
        ]
        distance = jnp.full(gathered.shape, SOFTEN_FAR, jnp.float32)
        for axis in range(3):
            gap = spot[axis] - centers[axis]
            distance = distance + gap * gap
        far[pl.ds(t, 1), :] = jnp.sum(
            gathered[...] * lax.rsqrt(distance), axis=0, keepdims=True
        )
        return carry

    lax.fori_loop(0, cells, far_cell, 0)
    lane = lax.broadcasted_iota(jnp.int32, (STEP, LANES), 1)

    def near_cell(t, carry):
        x, rest = lax.div(t, cy * cz), lax.rem(t, cy * cz)
        y, z = lax.div(rest, cz), lax.rem(rest, cz)
        sources = [
            (t, None, 0.0),
            (jnp.where(x < cx - 1, t + cy * cz, base[0] + face[0] + y * cz + z), 0, 1.0),
            (jnp.where(x > 0, t - cy * cz, base[0] + y * cz + z), 0, -1.0),
            (jnp.where(y < cy - 1, t + cz, base[1] + face[1] + x * cz + z), 1, 1.0),
            (jnp.where(y > 0, t - cz, base[1] + x * cz + z), 1, -1.0),
            (jnp.where(z < cz - 1, t + 1, base[2] + face[2] + x * cy + y), 2, 1.0),
            (jnp.where(z > 0, t - 1, base[2] + x * cy + y), 2, -1.0),
        ]
        for k, (row, axis, shift) in enumerate(sources):
            for c in range(9):
                value = ext[c, pl.ds(row, 1), :]
                if k == 0:
                    rows[c : c + 1, :] = value
                if c == axis:
                    value = value + shift
                staged[k * 9 + c] = jnp.broadcast_to(value, (8, LANES))
        turned[...] = rows[...].T
        count = counts[t]

        def chunk(i, carry):
            start = pl.multiple_of(i * STEP, STEP)
            tile = turned[pl.ds(start, STEP), :]
            mine = [
                [jnp.broadcast_to(tile[8 * h : 8 * h + 8, c : c + 1], (8, LANES)) for c in range(9)]
                for h in range(STEP // 8)
            ]
            total = [[jnp.zeros((8, LANES), jnp.float32)] * 3 for _ in range(STEP // 8)]
            for k in range(7):
                other = [staged[k * 9 + c] for c in range(9)]
                for h in range(STEP // 8):
                    me = mine[h]
                    d = [me[c] - other[c] for c in range(3)]
                    radius = d[0] * d[0] + d[1] * d[1] + d[2] * d[2] + SOFTEN_NEAR
                    inverse = lax.rsqrt(radius)
                    bb = me[3] * other[3] + me[4] * other[4] + me[5] * other[5]
                    ll = me[6] * other[6] + me[7] * other[7] + me[8] * other[8]
                    weight = (bb * ll) * (inverse * inverse * inverse)
                    total[h] = [total[h][c] + weight * d[c] for c in range(3)]
            for h in range(STEP // 8):
                out = jnp.zeros((8, LANES), jnp.float32)
                for c in range(3):
                    out = jnp.where(
                        lane[0:8] == c, jnp.sum(total[h][c], axis=1, keepdims=True), out
                    )
                sums[pl.ds(start + 8 * h, 8), :] = out
            return carry

        lax.fori_loop(0, lax.div(count + STEP - 1, STEP), chunk, 0)
        flipped = sums[...].T
        alive = lane[0:1] < count
        for c in range(3):
            near[c, pl.ds(t, 1), :] = jnp.where(alive, flipped[c : c + 1, :], 0.0)
        return carry

    rows[...] = jnp.zeros_like(rows)
    sums[...] = jnp.zeros_like(sums)
    lax.fori_loop(0, cells, near_cell, 0)

    mixed = jnp.dot(
        far[...], groups[...], precision=lax.Precision.HIGHEST, preferred_element_type=jnp.float32
    )
    burgers = [stacked[3 + c] for c in range(3)]
    line = [stacked[6 + c] for c in range(3)]
    pulled = []
    for r in range(3):
        value = 0.0
        for c in range(3):
            sigma = FAR_SCALE * mixed[:, 3 * r + c : 3 * r + c + 1] + stress[r, c]
            value = value + sigma * burgers[c]
        pulled.append(value)
    for c in range(3):
        a, b = (c + 1) % 3, (c + 2) % 3
        total = NEAR_SCALE * near[c] + (pulled[a] * line[b] - pulled[b] * line[a])
        near[c] = 0.5 * total

    node_rows = pos.shape[1]
    half = node_rows // 2
    acc[...] = jnp.zeros_like(acc)
    high_ids = lax.broadcasted_iota(jnp.int32, (half, LANES), 0)
    low_ids = lax.broadcasted_iota(jnp.int32, (2 * LANES, LANES), 0)
    groups_of = cells // 8

    def scatter(step, carry):
        end, block = lax.div(step, groups_of), lax.rem(step, groups_of)
        start = pl.multiple_of(block * 8, 8)
        ids = connect[end, pl.ds(start, 8), :]
        values = [near[c, pl.ds(start, 8), :] for c in range(3)]
        node_row = lax.shift_right_logical(ids, 7)
        upper = node_row >= half
        hi = jnp.where(upper, node_row - half, node_row)
        lo = (ids & (LANES - 1)) + jnp.where(upper, LANES, 0)
        for k in range(8):
            span = slice(k * LANES, (k + 1) * LANES)
            mask = high_ids == hi[k : k + 1, :]
            for c in range(3):
                value = values[c][k : k + 1, :]
                coarse = value.astype(jnp.bfloat16).astype(jnp.float32)
                fine = value - coarse
                left[2 * c * half : (2 * c + 1) * half, span] = jnp.where(mask, coarse, 0.0).astype(
                    jnp.bfloat16
                )
                left[(2 * c + 1) * half : (2 * c + 2) * half, span] = jnp.where(
                    mask, fine, 0.0
                ).astype(jnp.bfloat16)
            right[:, span] = jnp.where(low_ids == lo[k : k + 1, :], 1.0, 0.0).astype(jnp.bfloat16)
        acc[...] += lax.dot_general(
            left[...], right[...], (((1,), (1,)), ((), ())), preferred_element_type=jnp.float32
        )
        return carry

    lax.fori_loop(0, 2 * groups_of, scatter, 0)
    edge = low.shape[1]
    for c in range(3):
        both = acc[2 * c * half : (2 * c + 1) * half, :] + acc[(2 * c + 1) * half : (2 * c + 2) * half, :]
        for s in range(2):
            span = slice(s * half, (s + 1) * half)
            velocity = both[:, s * LANES : (s + 1) * LANES] / drag[span, :]
            fields[3 + c, span, :] = velocity
            fields[c, span, :] = pos[c, span, :] + TIME_STEP * velocity
    for c in range(6):
        low[c] = fields[c, 0:edge, :]
        high[c] = fields[c, node_rows - edge : node_rows, :]


def edge_kernel(n, low, high, below, above, send, recv):
    me = lax.axis_index("gx")
    barrier = pltpu.get_barrier_semaphore()
    after, before = lax.rem(me + 1, n), lax.rem(me + n - 1, n)
    for peer in (after, before):
        pl.semaphore_signal(barrier, inc=1, device_id={"gx": peer}, device_id_type=MESH)
    pl.semaphore_wait(barrier, 2)

    def copy(slot, src, dst, peer):
        return pltpu.make_async_remote_copy(
            src_ref=src,
            dst_ref=dst,
            send_sem=send.at[slot],
            recv_sem=recv.at[slot],
            device_id={"gx": peer},
            device_id_type=MESH,
        )

    @pl.when(me < n - 1)
    def _():
        copy(0, high, below, after).start()

    @pl.when(me > 0)
    def _():
        copy(1, low, above, before).start()

    @pl.when(me < n - 1)
    def _():
        copy(0, high, below, after).wait_send()
        copy(1, low, above, before).wait_recv()

    @pl.when(me > 0)
    def _():
        copy(1, low, above, before).wait_send()
        copy(0, high, below, after).wait_recv()


def assemble_kernel(moves, fields, below, above, out, section):
    node_rows, edge, out_rows = fields.shape[1], below.shape[1], out.shape[1]
    nodes, margin = node_rows * LANES, edge * LANES
    section[:, 0:edge, :] = below[...]
    section[:, edge : edge + node_rows, :] = fields[...]
    section[:, edge + node_rows : 2 * edge + node_rows, :] = above[...]
    up_prev, down_own, up_own, down_next = moves[0], moves[1], moves[2], moves[3]
    kept = nodes - up_own - down_own

    def shifted(c, by, first, count):
        row, turn = lax.div(by, LANES), lax.rem(by, LANES)
        lane = lax.broadcasted_iota(jnp.int32, (count, LANES), 1)
        back = lax.rem(LANES - turn, LANES)
        now = pltpu.roll(section[c, pl.ds(first + row, count), :], back, axis=1)
        later = pltpu.roll(section[c, pl.ds(first + row + 1, count), :], back, axis=1)
        return jnp.where(lane < LANES - turn, now, later)

    tail = out_rows - (4 * edge)
    position = (
        lax.broadcasted_iota(jnp.int32, (out_rows, LANES), 0) * LANES
        + lax.broadcasted_iota(jnp.int32, (out_rows, LANES), 1)
    )
    for c in range(6):
        out[c] = shifted(c, margin + down_own - up_prev, 0, out_rows)
        head = 2 * edge
        value = shifted(c, margin - up_prev, 0, head)
        out[c, 0:head, :] = jnp.where(position[0:head] < up_prev, value, out[c, 0:head, :])
        value = shifted(c, margin + nodes - up_prev - kept, tail, out_rows - tail)
        spot = position[tail:]
        value = jnp.where(spot < up_prev + kept, out[c, tail:out_rows, :], value)
        out[c, tail:out_rows, :] = jnp.where(spot < up_prev + kept + down_next, value, 0.0)


def shards(mesh, offsets, burgers, lines, counts, connect, node_pos, drag, stress, shifts):
    grid = offsets.shape[1:4]
    slots = offsets.shape[4]
    cells = grid[0] * grid[1] * grid[2]
    sizes = tuple(mesh.shape[name] for name in AXES)
    nx, ny, nz = sizes
    devices = nx * ny * nz
    index = [lax.axis_index(name) for name in AXES]
    half = [size // 2 for size in grid]
    local = half[0] * half[1] * half[2]
    nodes = node_pos.shape[4]
    node_rows, edge = nodes // LANES, MIG // LANES
    f32 = jnp.float32

    t = np.arange(cells)
    x, y, z = t // (grid[1] * grid[2]), t // grid[2] % grid[1], t % grid[2]
    coarse = ((x // 2) * half[1] + y // 2) * half[2] + z // 2
    lane = np.arange(LANES)
    code = np.where(lane[None, :] % local == coarse[:, None], lane[None, :] // local, -1)
    device = np.arange(devices)[:, None]
    inner = (lane % local)[None, :]
    centers = np.stack(
        [
            2 * (device // (ny * nz) * half[0] + inner // (half[1] * half[2])) + 1,
            2 * (device // nz % ny * half[1] + inner // half[2] % half[1]) + 1,
            2 * (device % nz * half[2] + inner % half[2]) + 1,
        ]
    ).astype(np.float32)
    groups = (lane[:, None] // local == lane[None, :]).astype(np.float32)

    flat = lambda array: array.reshape(array.shape[0], cells, slots)
    count_rows = counts.reshape(cells)
    face = (grid[1] * grid[2], grid[0] * grid[2], grid[0] * grid[1])
    face_shapes = [jax.ShapeDtypeStruct((2, 9, size, slots), f32) for size in face]

    stacked, fx, fy, fz, moments = pl.pallas_call(
        functools.partial(prep_kernel, grid),
        out_shape=[jax.ShapeDtypeStruct((9, cells, slots), f32)]
        + face_shapes
        + [jax.ShapeDtypeStruct((1, LANES), f32)],
        in_specs=[VM] * 5,
        out_specs=[VM] * 5,
        name="prep",
    )(
        flat(offsets), flat(burgers), flat(lines),
        jnp.broadcast_to(count_rows[:, None], (cells, LANES)), jnp.asarray(code, jnp.int32),
    )

    steps = sum(sizes) - 3
    hx, hy, hz, gathered = pl.pallas_call(
        functools.partial(exchange_kernel, sizes),
        out_shape=face_shapes + [jax.ShapeDtypeStruct((devices, 1, LANES), f32)],
        in_specs=[VM] * 4,
        out_specs=[VM] * 4,
        scratch_shapes=[
            pltpu.SemaphoreType.DMA((6,)),
            pltpu.SemaphoreType.DMA((6,)),
            pltpu.SemaphoreType.DMA((steps,)),
            pltpu.SemaphoreType.DMA((steps,)),
            pltpu.SemaphoreType.DMA,
        ],
        compiler_params=pltpu.CompilerParams(collective_id=0, has_side_effects=True),
        name="exchange",
    )(fx, fy, fz, moments.reshape(1, 1, LANES))

    edge_shape = jax.ShapeDtypeStruct((6, edge, LANES), f32)
    fields, low, high = pl.pallas_call(
        functools.partial(force_kernel, grid, sizes),
        out_shape=[jax.ShapeDtypeStruct((6, node_rows, LANES), f32), edge_shape, edge_shape],
        in_specs=[SM] * 3 + [VM] * 10,
        out_specs=[VM] * 3,
        scratch_shapes=[
            pltpu.VMEM((9, cells + 2 * sum(face), LANES), f32),
            pltpu.VMEM((63, 8, LANES), f32),
            pltpu.VMEM((16, LANES), f32),
            pltpu.VMEM((LANES, 16), f32),
            pltpu.VMEM((LANES, LANES), f32),
            pltpu.VMEM((3, cells, LANES), f32),
            pltpu.VMEM((cells, LANES), f32),
            pltpu.VMEM((3 * node_rows, 8 * LANES), jnp.bfloat16),
            pltpu.VMEM((2 * LANES, 8 * LANES), jnp.bfloat16),
            pltpu.VMEM((3 * node_rows, 2 * LANES), f32),
        ],
        name="forces",
    )(
        count_rows, jnp.stack(index).astype(jnp.int32), stress,
        stacked, hx, hy, hz, gathered.reshape(devices, LANES),
        jnp.asarray(centers), jnp.asarray(groups),
        flat(connect), node_pos.reshape(3, node_rows, LANES), drag.reshape(node_rows, LANES),
    )

    below, above = pl.pallas_call(
        functools.partial(edge_kernel, nx),
        out_shape=[edge_shape, edge_shape],
        in_specs=[VM] * 2,
        out_specs=[VM] * 2,
        scratch_shapes=[pltpu.SemaphoreType.DMA((2,)), pltpu.SemaphoreType.DMA((2,))],
        compiler_params=pltpu.CompilerParams(collective_id=1, has_side_effects=True),
        name="edges",
    )(low, high)

    ix, iy, iz = index
    up_prev = jnp.where(ix > 0, shifts[0][jnp.maximum(ix - 1, 0), iy, iz], 0)
    down_next = jnp.where(ix < nx - 1, shifts[1][jnp.minimum(ix + 1, nx - 1), iy, iz], 0)
    moves = jnp.stack([up_prev, shifts[1][ix, iy, iz], shifts[0][ix, iy, iz], down_next])
    out_rows = node_rows + 2 * edge
    result = pl.pallas_call(
        assemble_kernel,
        out_shape=jax.ShapeDtypeStruct((6, out_rows, LANES), f32),
        in_specs=[SM] + [VM] * 3,
        out_specs=VM,
        scratch_shapes=[pltpu.VMEM((6, out_rows + 4 * edge, LANES), f32)],
        name="assemble",
    )(moves.astype(jnp.int32), fields, below, above)
    return result.reshape(6, 1, 1, 1, out_rows * LANES)


def solution(mesh):
    return jax.shard_map(
        functools.partial(shards, mesh),
        mesh=mesh,
        in_specs=(
            P(None, "gx", "gy", "gz", None),
            P(None, "gx", "gy", "gz", None),
            P(None, "gx", "gy", "gz", None),
            P("gx", "gy", "gz"),
            P(None, "gx", "gy", "gz", None),
            P(None, "gx", "gy", "gz", None),
            P("gx", "gy", "gz", None),
            P(),
            P(),
        ),
        out_specs=P(None, "gx", "gy", "gz", None),
        check_vma=False,
    )
```

```python
import functools

import jax
import jax.numpy as jnp
import numpy as np
from jax import lax
from jax.experimental import pallas as pl
from jax.experimental.pallas import tpu as pltpu
from jax.sharding import PartitionSpec as P

MIG = 512
SOFTEN_NEAR = 0.25
SOFTEN_FAR = 4.0
NEAR_SCALE = 0.0625
FAR_SCALE = 0.03125
TIME_STEP = 0.1
AXES = ("gx", "gy", "gz")
MESH = pl.DeviceIdType.MESH
VM = pl.BlockSpec(memory_space=pltpu.VMEM)
SM = pl.BlockSpec(memory_space=pltpu.SMEM)
LANES = 128
STEP = 16
ROWS = 16


def prep_kernel(grid, off, bur, lin, counts, code, stacked, faces_x, faces_y, faces_z, mom):
    cx, cy, cz = grid
    cells = cx * cy * cz
    live = lax.broadcasted_iota(jnp.int32, (cells, LANES), 1) < counts[...]
    for c in range(3):
        stacked[c] = off[c]
        stacked[3 + c] = jnp.where(live, bur[c], 0.0)
        stacked[6 + c] = lin[c]
    for c in range(9):
        faces_x[0, c] = stacked[c, 0 : cy * cz, :]
        faces_x[1, c] = stacked[c, cells - cy * cz : cells, :]
        for x in range(cx):
            base = x * cy * cz
            faces_y[0, c, x * cz : (x + 1) * cz, :] = stacked[c, base : base + cz, :]
            base = base + (cy - 1) * cz
            faces_y[1, c, x * cz : (x + 1) * cz, :] = stacked[c, base : base + cz, :]
        faces_z[0, c] = stacked[c, pl.ds(0, cx * cy, stride=cz), :]
        faces_z[1, c] = stacked[c, pl.ds(cz - 1, cx * cy, stride=cz), :]
    total = jnp.zeros((cells, LANES), jnp.float32)
    for a in range(3):
        for b in range(3):
            part = jnp.sum(stacked[3 + a] * stacked[6 + b], axis=1, keepdims=True)
            total = total + jnp.where(code[...] == 3 * a + b, part, 0.0)
    mom[...] = jnp.sum(total, axis=0, keepdims=True)


def exchange_kernel(sizes, fx, fy, fz, mom, hx, hy, hz, gathered, *sems):
    face_send, face_recv, mom_send, mom_recv, own_sem = sems
    index = [lax.axis_index(name) for name in AXES]
    barrier = pltpu.get_barrier_semaphore()
    peers = 0
    for name, me, n in zip(AXES, index, sizes):
        for d in range(1, n):
            pl.semaphore_signal(
                barrier, inc=1, device_id={name: lax.rem(me + d, n)}, device_id_type=MESH
            )
            peers += 1
    pl.semaphore_wait(barrier, peers)

    def moment_copies(level, src, dst):
        name, me, n = AXES[level], index[level], sizes[level]
        base = sum(size - 1 for size in sizes[:level])
        return [
            pltpu.make_async_remote_copy(
                src_ref=src,
                dst_ref=dst,
                send_sem=mom_send.at[base + d - 1],
                recv_sem=mom_recv.at[base + d - 1],
                device_id={name: lax.rem(me + d, n)},
                device_id_type=MESH,
            )
            for d in range(1, n)
        ]

    nx, ny, nz = sizes
    row = (index[0] * ny + index[1]) * nz + index[2]
    own = pltpu.make_async_copy(mom, gathered.at[pl.ds(row, 1)], own_sem)
    own.start()
    first = moment_copies(2, mom, gathered.at[pl.ds(row, 1)])
    for copy in first:
        copy.start()

    def face_copy(axis, face, halo, up):
        me, n = index[axis], sizes[axis]
        slot = 2 * axis + (0 if up else 1)
        return pltpu.make_async_remote_copy(
            src_ref=face.at[1 if up else 0],
            dst_ref=halo.at[0 if up else 1],
            send_sem=face_send.at[slot],
            recv_sem=face_recv.at[slot],
            device_id={AXES[axis]: lax.rem(me + 1, n) if up else lax.rem(me + n - 1, n)},
            device_id_type=MESH,
        )

    pairs = [(0, fx, hx), (1, fy, hy), (2, fz, hz)]

    def start_faces(axis, face, halo):
        @pl.when(index[axis] < sizes[axis] - 1)
        def _():
            face_copy(axis, face, halo, True).start()

        @pl.when(index[axis] > 0)
        def _():
            face_copy(axis, face, halo, False).start()

    for axis, face, halo in pairs:
        start_faces(axis, face, halo)
    own.wait()
    for copy in first:
        copy.wait_recv()
    block = gathered.at[pl.ds((index[0] * ny + index[1]) * nz, nz)]
    second = moment_copies(1, block, block)
    for copy in second:
        copy.start()
    for copy in second:
        copy.wait_recv()
    block = gathered.at[pl.ds(index[0] * ny * nz, ny * nz)]
    third = moment_copies(0, block, block)
    for copy in third:
        copy.start()
    for copy in third:
        copy.wait_recv()
    for axis, face, halo in pairs:

        @pl.when(index[axis] > 0)
        def _():
            face_copy(axis, face, halo, True).wait_recv()

        @pl.when(index[axis] < sizes[axis] - 1)
        def _():
            face_copy(axis, face, halo, False).wait_recv()

        @pl.when(index[axis] < sizes[axis] - 1)
        def _():
            face_copy(axis, face, halo, True).wait_send()

        @pl.when(index[axis] > 0)
        def _():
            face_copy(axis, face, halo, False).wait_send()

    for copy in first + second + third:
        copy.wait_send()


def force_kernel(
    grid, sizes, counts, stress, stacked, hx, hy, hz, gathered, centers, groups,
    connect, pos, drag, fields, low, high, ext, packed, staged, turned, sums, near, far, left, right, acc,
):
    cx, cy, cz = grid
    cells = cx * cy * cz
    where = [lax.axis_index(name) for name in AXES]
    face = (cy * cz, cx * cz, cx * cy)
    base = [cells]
    for axis in range(3):
        base.append(base[-1] + 2 * face[axis])
    for c in range(9):
        ext[pl.ds(c, cells, stride=ROWS), :] = stacked[c]
        for axis, halo in enumerate((hx, hy, hz)):
            for side in range(2):
                start = base[axis] + side * face[axis]
                ext[pl.ds(start * ROWS + c, face[axis], stride=ROWS), :] = halo[side, c]
    full = ext.shape[1]
    outer = [
        (
            jnp.where(where[axis] > 0, full, 0),
            jnp.where(where[axis] < sizes[axis] - 1, full, 0),
        )
        for axis in range(3)
    ]

    def far_cell(t, carry):
        x, rest = lax.div(t, cy * cz), lax.rem(t, cy * cz)
        y, z = lax.div(rest, cz), lax.rem(rest, cz)
        spot = [
            (where[axis] * grid[axis] + (x, y, z)[axis]).astype(jnp.float32) + 0.5
            for axis in range(3)
        ]
        distance = jnp.full(gathered.shape, SOFTEN_FAR, jnp.float32)
        for axis in range(3):
            gap = spot[axis] - centers[axis]
            distance = distance + gap * gap
        far[pl.ds(t, 1), :] = jnp.sum(
            gathered[...] * lax.rsqrt(distance), axis=0, keepdims=True
        )
        return carry

    lax.fori_loop(0, cells, far_cell, 0)
    lane = lax.broadcasted_iota(jnp.int32, (ROWS, LANES), 1)
    sub = lax.broadcasted_iota(jnp.int32, (ROWS, LANES), 0)

    def near_cell(t, carry):
        x, rest = lax.div(t, cy * cz), lax.rem(t, cy * cz)
        y, z = lax.div(rest, cz), lax.rem(rest, cz)
        spot = (x, y, z)
        count = counts[t]
        mine_tile = ext[pl.ds(pl.multiple_of(t * ROWS, ROWS), ROWS), :]
        turned[...] = mine_tile.T
        sources = [(t, count, None, 0.0)]
        pitch = (cy * cz, cz, 1)
        offset = (y * cz + z, x * cz + z, x * cy + y)
        for axis in range(3):
            for side, step in ((1, 1.0), (0, -1.0)):
                inner = spot[axis] < grid[axis] - 1 if side else spot[axis] > 0
                beside = t + pitch[axis] if side else t - pitch[axis]
                beside = jnp.where(inner, beside, 0)
                row = jnp.where(inner, beside, base[axis] + side * face[axis] + offset[axis])
                number = jnp.where(inner, counts[beside], outer[axis][side])
                sources.append((row, number, axis, step))
        for q in range(packed.shape[0]):
            packed[q] = jnp.zeros((ROWS, LANES), jnp.float32)
        fill = jnp.int32(0)
        for row, number, axis, step in sources:
            tile = ext[pl.ds(pl.multiple_of(row * ROWS, ROWS), ROWS), :]
            if axis is not None:
                tile = jnp.where(sub == axis, tile + step, tile)
            turn, q = lax.rem(fill, LANES), lax.div(fill, LANES)
            rolled = pltpu.roll(tile, turn, axis=1)
            packed[q] += jnp.where((lane >= turn) & (lane < turn + number), rolled, 0.0)
            packed[q + 1] += jnp.where(lane < turn + number - LANES, rolled, 0.0)
            fill = fill + number
        used = lax.div(fill + LANES - 1, LANES)

        def spread(q, carry):
            for c in range(9):
                staged[q * 9 + c] = jnp.broadcast_to(packed[q, c : c + 1, :], (8, LANES))
            return carry

        lax.fori_loop(0, used, spread, 0)

        def chunk(n, i, carry):
            start = pl.multiple_of(i * STEP, STEP)
            tile = turned[pl.ds(start, STEP), :]
            mine = [
                [jnp.broadcast_to(tile[8 * h : 8 * h + 8, c : c + 1], (8, LANES)) for c in range(9)]
                for h in range(STEP // 8)
            ]
            total = [[None] * 3 for _ in range(STEP // 8)]
            for k in range(n):
                other = [staged[k * 9 + c] for c in range(9)]
                for h in range(STEP // 8):
                    me = mine[h]
                    d = [me[c] - other[c] for c in range(3)]
                    radius = d[0] * d[0] + d[1] * d[1] + d[2] * d[2] + SOFTEN_NEAR
                    inverse = lax.rsqrt(radius)
                    bb = me[3] * other[3] + me[4] * other[4] + me[5] * other[5]
                    ll = me[6] * other[6] + me[7] * other[7] + me[8] * other[8]
                    weight = (bb * ll) * (inverse * inverse * inverse)
                    for c in range(3):
                        term = weight * d[c]
                        total[h][c] = term if k == 0 else total[h][c] + term
            for h in range(STEP // 8):
                out = jnp.zeros((8, LANES), jnp.float32)
                for c in range(3):
                    out = jnp.where(
                        lane[0:8] == c, jnp.sum(total[h][c], axis=1, keepdims=True), out
                    )
                sums[pl.ds(start + 8 * h, 8), :] = out[:, 0:8]
            return carry

        chunks = lax.div(count + STEP - 1, STEP)
        for n in range(1, 8):

            @pl.when(used == n)
            def _():
                lax.fori_loop(0, chunks, functools.partial(chunk, n), 0)

        flipped = sums[...].T
        alive = lane[0:1] < count
        for c in range(3):
            near[c, pl.ds(t, 1), :] = jnp.where(alive, flipped[c : c + 1, :], 0.0)
        return carry

    sums[...] = jnp.zeros_like(sums)
    lax.fori_loop(0, cells, near_cell, 0)

    mixed = jnp.dot(
        far[...], groups[...], precision=lax.Precision.HIGHEST, preferred_element_type=jnp.float32
    )
    burgers = [stacked[3 + c] for c in range(3)]
    line = [stacked[6 + c] for c in range(3)]
    pulled = []
    for r in range(3):
        value = 0.0
        for c in range(3):
            sigma = FAR_SCALE * mixed[:, 3 * r + c : 3 * r + c + 1] + stress[r, c]
            value = value + sigma * burgers[c]
        pulled.append(value)
    for c in range(3):
        a, b = (c + 1) % 3, (c + 2) % 3
        total = NEAR_SCALE * near[c] + (pulled[a] * line[b] - pulled[b] * line[a])
        near[c] = 0.5 * total

    node_rows = pos.shape[1]
    half = node_rows // 2
    acc[...] = jnp.zeros_like(acc)
    high_ids = lax.broadcasted_iota(jnp.int32, (half, LANES), 0)
    low_ids = lax.broadcasted_iota(jnp.int32, (2 * LANES, LANES), 0)
    groups_of = cells // 8

    def scatter(step, carry):
        end, block = lax.div(step, groups_of), lax.rem(step, groups_of)
        start = pl.multiple_of(block * 8, 8)
        ids = connect[end, pl.ds(start, 8), :]
        values = [near[c, pl.ds(start, 8), :] for c in range(3)]
        node_row = lax.shift_right_logical(ids, 7)
        upper = node_row >= half
        hi = jnp.where(upper, node_row - half, node_row)
        lo = (ids & (LANES - 1)) + jnp.where(upper, LANES, 0)
        for k in range(8):
            span = slice(k * LANES, (k + 1) * LANES)
            mask = high_ids == hi[k : k + 1, :]
            for c in range(3):
                value = values[c][k : k + 1, :]
                coarse = value.astype(jnp.bfloat16).astype(jnp.float32)
                fine = value - coarse
                left[2 * c * half : (2 * c + 1) * half, span] = jnp.where(mask, coarse, 0.0).astype(
                    jnp.bfloat16
                )
                left[(2 * c + 1) * half : (2 * c + 2) * half, span] = jnp.where(
                    mask, fine, 0.0
                ).astype(jnp.bfloat16)
            right[:, span] = jnp.where(low_ids == lo[k : k + 1, :], 1.0, 0.0).astype(jnp.bfloat16)
        acc[...] += lax.dot_general(
            left[...], right[...], (((1,), (1,)), ((), ())), preferred_element_type=jnp.float32
        )
        return carry

    lax.fori_loop(0, 2 * groups_of, scatter, 0)
    edge = low.shape[1]
    for c in range(3):
        both = acc[2 * c * half : (2 * c + 1) * half, :] + acc[(2 * c + 1) * half : (2 * c + 2) * half, :]
        for s in range(2):
            span = slice(s * half, (s + 1) * half)
            velocity = both[:, s * LANES : (s + 1) * LANES] / drag[span, :]
            fields[3 + c, span, :] = velocity
            fields[c, span, :] = pos[c, span, :] + TIME_STEP * velocity
    for c in range(6):
        low[c] = fields[c, 0:edge, :]
        high[c] = fields[c, node_rows - edge : node_rows, :]


def edge_kernel(n, low, high, below, above, send, recv):
    me = lax.axis_index("gx")
    barrier = pltpu.get_barrier_semaphore()
    after, before = lax.rem(me + 1, n), lax.rem(me + n - 1, n)
    for peer in (after, before):
        pl.semaphore_signal(barrier, inc=1, device_id={"gx": peer}, device_id_type=MESH)
    pl.semaphore_wait(barrier, 2)

    def copy(slot, src, dst, peer):
        return pltpu.make_async_remote_copy(
            src_ref=src,
            dst_ref=dst,
            send_sem=send.at[slot],
            recv_sem=recv.at[slot],
            device_id={"gx": peer},
            device_id_type=MESH,
        )

    @pl.when(me < n - 1)
    def _():
        copy(0, high, below, after).start()

    @pl.when(me > 0)
    def _():
        copy(1, low, above, before).start()

    @pl.when(me < n - 1)
    def _():
        copy(0, high, below, after).wait_send()
        copy(1, low, above, before).wait_recv()

    @pl.when(me > 0)
    def _():
        copy(1, low, above, before).wait_send()
        copy(0, high, below, after).wait_recv()


def assemble_kernel(sizes, moves, fields, below, above, out, section):
    node_rows, edge, out_rows = fields.shape[1], below.shape[1], out.shape[1]
    nodes, margin = node_rows * LANES, edge * LANES
    section[:, 0:edge, :] = below[...]
    section[:, edge : edge + node_rows, :] = fields[...]
    section[:, edge + node_rows : 2 * edge + node_rows, :] = above[...]
    nx, ny, nz = sizes
    ix, iy, iz = [lax.axis_index(name) for name in AXES]
    at = lambda k, slab: moves[((k * nx + slab) * ny + iy) * nz + iz]
    up_own, down_own = at(0, ix), at(1, ix)
    up_prev = jnp.where(ix > 0, at(0, jnp.maximum(ix - 1, 0)), 0)
    down_next = jnp.where(ix < nx - 1, at(1, jnp.minimum(ix + 1, nx - 1)), 0)
    kept = nodes - up_own - down_own

    def shifted(c, by, first, count):
        row, turn = lax.div(by, LANES), lax.rem(by, LANES)
        lane = lax.broadcasted_iota(jnp.int32, (count, LANES), 1)
        back = lax.rem(LANES - turn, LANES)
        now = pltpu.roll(section[c, pl.ds(first + row, count), :], back, axis=1)
        later = pltpu.roll(section[c, pl.ds(first + row + 1, count), :], back, axis=1)
        return jnp.where(lane < LANES - turn, now, later)

    tail = out_rows - (4 * edge)
    position = (
        lax.broadcasted_iota(jnp.int32, (out_rows, LANES), 0) * LANES
        + lax.broadcasted_iota(jnp.int32, (out_rows, LANES), 1)
    )
    for c in range(6):
        out[c] = shifted(c, margin + down_own - up_prev, 0, out_rows)
        head = 2 * edge
        value = shifted(c, margin - up_prev, 0, head)
        out[c, 0:head, :] = jnp.where(position[0:head] < up_prev, value, out[c, 0:head, :])
        value = shifted(c, margin + nodes - up_prev - kept, tail, out_rows - tail)
        spot = position[tail:]
        value = jnp.where(spot < up_prev + kept, out[c, tail:out_rows, :], value)
        out[c, tail:out_rows, :] = jnp.where(spot < up_prev + kept + down_next, value, 0.0)


def shards(mesh, offsets, burgers, lines, counts, connect, node_pos, drag, stress, shifts):
    grid = offsets.shape[1:4]
    slots = offsets.shape[4]
    cells = grid[0] * grid[1] * grid[2]
    sizes = tuple(mesh.shape[name] for name in AXES)
    nx, ny, nz = sizes
    devices = nx * ny * nz
    half = [size // 2 for size in grid]
    local = half[0] * half[1] * half[2]
    nodes = node_pos.shape[4]
    node_rows, edge = nodes // LANES, MIG // LANES
    f32 = jnp.float32

    t = np.arange(cells)
    x, y, z = t // (grid[1] * grid[2]), t // grid[2] % grid[1], t % grid[2]
    coarse = ((x // 2) * half[1] + y // 2) * half[2] + z // 2
    lane = np.arange(LANES)
    code = np.where(lane[None, :] % local == coarse[:, None], lane[None, :] // local, -1)
    device = np.arange(devices)[:, None]
    inner = (lane % local)[None, :]
    centers = np.stack(
        [
            2 * (device // (ny * nz) * half[0] + inner // (half[1] * half[2])) + 1,
            2 * (device // nz % ny * half[1] + inner // half[2] % half[1]) + 1,
            2 * (device % nz * half[2] + inner % half[2]) + 1,
        ]
    ).astype(np.float32)
    groups = (lane[:, None] // local == lane[None, :]).astype(np.float32)

    flat = lambda array: array.reshape(array.shape[0], cells, slots)
    count_rows = counts.reshape(cells)
    face = (grid[1] * grid[2], grid[0] * grid[2], grid[0] * grid[1])
    face_shapes = [jax.ShapeDtypeStruct((2, 9, size, slots), f32) for size in face]

    stacked, fx, fy, fz, moments = pl.pallas_call(
        functools.partial(prep_kernel, grid),
        out_shape=[jax.ShapeDtypeStruct((9, cells, slots), f32)]
        + face_shapes
        + [jax.ShapeDtypeStruct((1, LANES), f32)],
        in_specs=[VM] * 5,
        out_specs=[VM] * 5,
        name="prep",
    )(
        flat(offsets), flat(burgers), flat(lines),
        jnp.broadcast_to(count_rows[:, None], (cells, LANES)), jnp.asarray(code, jnp.int32),
    )

    steps = sum(sizes) - 3
    hx, hy, hz, gathered = pl.pallas_call(
        functools.partial(exchange_kernel, sizes),
        out_shape=face_shapes + [jax.ShapeDtypeStruct((devices, 1, LANES), f32)],
        in_specs=[VM] * 4,
        out_specs=[VM] * 4,
        scratch_shapes=[
            pltpu.SemaphoreType.DMA((6,)),
            pltpu.SemaphoreType.DMA((6,)),
            pltpu.SemaphoreType.DMA((steps,)),
            pltpu.SemaphoreType.DMA((steps,)),
            pltpu.SemaphoreType.DMA,
        ],
        compiler_params=pltpu.CompilerParams(collective_id=0, has_side_effects=True),
        name="exchange",
    )(fx, fy, fz, moments.reshape(1, 1, LANES))

    edge_shape = jax.ShapeDtypeStruct((6, edge, LANES), f32)
    fields, low, high = pl.pallas_call(
        functools.partial(force_kernel, grid, sizes),
        out_shape=[jax.ShapeDtypeStruct((6, node_rows, LANES), f32), edge_shape, edge_shape],
        in_specs=[SM] * 2 + [VM] * 10,
        out_specs=[VM] * 3,
        scratch_shapes=[
            pltpu.VMEM(((cells + 2 * sum(face)) * ROWS, LANES), f32),
            pltpu.VMEM((8, ROWS, LANES), f32),
            pltpu.VMEM((63, 8, LANES), f32),
            pltpu.VMEM((LANES, ROWS), f32),
            pltpu.VMEM((LANES, 8), f32),
            pltpu.VMEM((3, cells, LANES), f32),
            pltpu.VMEM((cells, LANES), f32),
            pltpu.VMEM((3 * node_rows, 8 * LANES), jnp.bfloat16),
            pltpu.VMEM((2 * LANES, 8 * LANES), jnp.bfloat16),
            pltpu.VMEM((3 * node_rows, 2 * LANES), f32),
        ],
        name="forces",
    )(
        count_rows, stress,
        stacked, hx, hy, hz, gathered.reshape(devices, LANES),
        jnp.asarray(centers), jnp.asarray(groups),
        flat(connect), node_pos.reshape(3, node_rows, LANES), drag.reshape(node_rows, LANES),
    )

    below, above = pl.pallas_call(
        functools.partial(edge_kernel, nx),
        out_shape=[edge_shape, edge_shape],
        in_specs=[VM] * 2,
        out_specs=[VM] * 2,
        scratch_shapes=[pltpu.SemaphoreType.DMA((2,)), pltpu.SemaphoreType.DMA((2,))],
        compiler_params=pltpu.CompilerParams(collective_id=1, has_side_effects=True),
        name="edges",
    )(low, high)

    out_rows = node_rows + 2 * edge
    result = pl.pallas_call(
        functools.partial(assemble_kernel, sizes),
        out_shape=jax.ShapeDtypeStruct((6, out_rows, LANES), f32),
        in_specs=[SM] + [VM] * 3,
        out_specs=VM,
        scratch_shapes=[pltpu.VMEM((6, out_rows + 4 * edge, LANES), f32)],
        name="assemble",
    )(shifts.reshape(-1), fields, below, above)
    return result.reshape(6, 1, 1, 1, out_rows * LANES)


def solution(mesh):
    return jax.shard_map(
        functools.partial(shards, mesh),
        mesh=mesh,
        in_specs=(
            P(None, "gx", "gy", "gz", None),
            P(None, "gx", "gy", "gz", None),
            P(None, "gx", "gy", "gz", None),
            P("gx", "gy", "gz"),
            P(None, "gx", "gy", "gz", None),
            P(None, "gx", "gy", "gz", None),
            P("gx", "gy", "gz", None),
            P(),
            P(),
        ),
        out_specs=P(None, "gx", "gy", "gz", None),
        check_vma=False,
    )
```

```python
import functools

import jax
import jax.numpy as jnp
import numpy as np
from jax import lax
from jax.experimental import pallas as pl
from jax.experimental.pallas import tpu as pltpu
from jax.sharding import PartitionSpec as P

MIG = 512
SOFTEN_NEAR = 0.25
SOFTEN_FAR = 4.0
NEAR_SCALE = 0.0625
FAR_SCALE = 0.03125
TIME_STEP = 0.1
AXES = ("gx", "gy", "gz")
MESH = pl.DeviceIdType.MESH
VM = pl.BlockSpec(memory_space=pltpu.VMEM)
SM = pl.BlockSpec(memory_space=pltpu.SMEM)
LANES = 128
STEP = 16
ROWS = 16


def prep_kernel(grid, off, bur, lin, counts, code, stacked, faces_x, faces_y, faces_z, mom):
    cx, cy, cz = grid
    cells = cx * cy * cz
    live = lax.broadcasted_iota(jnp.int32, (cells, LANES), 1) < counts[...]
    for c in range(3):
        stacked[c] = off[c]
        stacked[3 + c] = jnp.where(live, bur[c], 0.0)
        stacked[6 + c] = lin[c]
    for c in range(9):
        faces_x[0, c] = stacked[c, 0 : cy * cz, :]
        faces_x[1, c] = stacked[c, cells - cy * cz : cells, :]
        for x in range(cx):
            base = x * cy * cz
            faces_y[0, c, x * cz : (x + 1) * cz, :] = stacked[c, base : base + cz, :]
            base = base + (cy - 1) * cz
            faces_y[1, c, x * cz : (x + 1) * cz, :] = stacked[c, base : base + cz, :]
        faces_z[0, c] = stacked[c, pl.ds(0, cx * cy, stride=cz), :]
        faces_z[1, c] = stacked[c, pl.ds(cz - 1, cx * cy, stride=cz), :]
    total = jnp.zeros((cells, LANES), jnp.float32)
    for a in range(3):
        for b in range(3):
            part = jnp.sum(stacked[3 + a] * stacked[6 + b], axis=1, keepdims=True)
            total = total + jnp.where(code[...] == 3 * a + b, part, 0.0)
    mom[...] = jnp.sum(total, axis=0, keepdims=True)


def exchange_kernel(sizes, fx, fy, fz, mom, hx, hy, hz, gathered, *sems):
    face_send, face_recv, mom_send, mom_recv, own_sem = sems
    index = [lax.axis_index(name) for name in AXES]
    barrier = pltpu.get_barrier_semaphore()
    peers = 0
    for name, me, n in zip(AXES, index, sizes):
        for d in range(1, n):
            pl.semaphore_signal(
                barrier, inc=1, device_id={name: lax.rem(me + d, n)}, device_id_type=MESH
            )
            peers += 1
    pl.semaphore_wait(barrier, peers)

    def moment_copies(level, src, dst):
        name, me, n = AXES[level], index[level], sizes[level]
        base = sum(size - 1 for size in sizes[:level])
        return [
            pltpu.make_async_remote_copy(
                src_ref=src,
                dst_ref=dst,
                send_sem=mom_send.at[base + d - 1],
                recv_sem=mom_recv.at[base + d - 1],
                device_id={name: lax.rem(me + d, n)},
                device_id_type=MESH,
            )
            for d in range(1, n)
        ]

    nx, ny, nz = sizes
    row = (index[0] * ny + index[1]) * nz + index[2]
    own = pltpu.make_async_copy(mom, gathered.at[pl.ds(row, 1)], own_sem)
    own.start()
    first = moment_copies(2, mom, gathered.at[pl.ds(row, 1)])
    for copy in first:
        copy.start()

    def face_copy(axis, face, halo, up):
        me, n = index[axis], sizes[axis]
        slot = 2 * axis + (0 if up else 1)
        return pltpu.make_async_remote_copy(
            src_ref=face.at[1 if up else 0],
            dst_ref=halo.at[0 if up else 1],
            send_sem=face_send.at[slot],
            recv_sem=face_recv.at[slot],
            device_id={AXES[axis]: lax.rem(me + 1, n) if up else lax.rem(me + n - 1, n)},
            device_id_type=MESH,
        )

    pairs = [(0, fx, hx), (1, fy, hy), (2, fz, hz)]

    def start_faces(axis, face, halo):
        @pl.when(index[axis] < sizes[axis] - 1)
        def _():
            face_copy(axis, face, halo, True).start()

        @pl.when(index[axis] > 0)
        def _():
            face_copy(axis, face, halo, False).start()

    for axis, face, halo in pairs:
        start_faces(axis, face, halo)
    own.wait()
    for copy in first:
        copy.wait_recv()
    block = gathered.at[pl.ds((index[0] * ny + index[1]) * nz, nz)]
    second = moment_copies(1, block, block)
    for copy in second:
        copy.start()
    for copy in second:
        copy.wait_recv()
    block = gathered.at[pl.ds(index[0] * ny * nz, ny * nz)]
    third = moment_copies(0, block, block)
    for copy in third:
        copy.start()
    for copy in third:
        copy.wait_recv()
    for axis, face, halo in pairs:

        @pl.when(index[axis] > 0)
        def _():
            face_copy(axis, face, halo, True).wait_recv()

        @pl.when(index[axis] < sizes[axis] - 1)
        def _():
            face_copy(axis, face, halo, False).wait_recv()

        @pl.when(index[axis] < sizes[axis] - 1)
        def _():
            face_copy(axis, face, halo, True).wait_send()

        @pl.when(index[axis] > 0)
        def _():
            face_copy(axis, face, halo, False).wait_send()

    for copy in first + second + third:
        copy.wait_send()


def force_kernel(
    grid, sizes, counts, stress, stacked, hx, hy, hz, gathered, centers, groups,
    connect, pos, drag, fields, low, high, ext, staged, turned, sums, near, far, left, right, acc,
):
    cx, cy, cz = grid
    cells = cx * cy * cz
    where = [lax.axis_index(name) for name in AXES]
    face = (cy * cz, cx * cz, cx * cy)
    base = [cells]
    for axis in range(3):
        base.append(base[-1] + 2 * face[axis])
    for c in range(9):
        ext[pl.ds(c, cells, stride=ROWS), :] = stacked[c]
        for axis, halo in enumerate((hx, hy, hz)):
            for side in range(2):
                start = base[axis] + side * face[axis]
                ext[pl.ds(start * ROWS + c, face[axis], stride=ROWS), :] = halo[side, c]
    full = ext.shape[1]
    outer = [
        (
            jnp.where(where[axis] > 0, full, 0),
            jnp.where(where[axis] < sizes[axis] - 1, full, 0),
        )
        for axis in range(3)
    ]

    def far_cell(t, carry):
        x, rest = lax.div(t, cy * cz), lax.rem(t, cy * cz)
        y, z = lax.div(rest, cz), lax.rem(rest, cz)
        spot = [
            (where[axis] * grid[axis] + (x, y, z)[axis]).astype(jnp.float32) + 0.5
            for axis in range(3)
        ]
        distance = jnp.full(gathered.shape, SOFTEN_FAR, jnp.float32)
        for axis in range(3):
            gap = spot[axis] - centers[axis]
            distance = distance + gap * gap
        far[pl.ds(t, 1), :] = jnp.sum(
            gathered[...] * lax.rsqrt(distance), axis=0, keepdims=True
        )
        return carry

    lax.fori_loop(0, cells, far_cell, 0)
    lane = lax.broadcasted_iota(jnp.int32, (ROWS, LANES), 1)
    sub = lax.broadcasted_iota(jnp.int32, (ROWS, LANES), 0)

    def near_cell(t, carry):
        x, rest = lax.div(t, cy * cz), lax.rem(t, cy * cz)
        y, z = lax.div(rest, cz), lax.rem(rest, cz)
        spot = (x, y, z)
        count = counts[t]
        mine_tile = ext[pl.ds(pl.multiple_of(t * ROWS, ROWS), ROWS), :]
        turned[...] = mine_tile.T
        sources = [(t, count, None, 0.0)]
        pitch = (cy * cz, cz, 1)
        offset = (y * cz + z, x * cz + z, x * cy + y)
        for axis in range(3):
            for side, step in ((1, 1.0), (0, -1.0)):
                inner = spot[axis] < grid[axis] - 1 if side else spot[axis] > 0
                beside = t + pitch[axis] if side else t - pitch[axis]
                beside = jnp.where(inner, beside, 0)
                row = jnp.where(inner, beside, base[axis] + side * face[axis] + offset[axis])
                number = jnp.where(inner, counts[beside], outer[axis][side])
                sources.append((row, number, axis, step))
        fill = jnp.int32(0)
        starts, tiles = [], []
        for row, number, axis, step in sources:
            tile = ext[pl.ds(pl.multiple_of(row * ROWS, ROWS), ROWS), :]
            if axis is not None:
                tile = jnp.where(sub == axis, tile + step, tile)
            tiles.append(pltpu.roll(tile, lax.rem(fill, LANES), axis=1))
            starts.append(fill)
            fill = fill + number
        used = lax.div(fill + LANES - 1, LANES)
        for q in range(len(sources)):
            place = lane + q * LANES
            value = tiles[0]
            for k in range(1, len(sources)):
                value = jnp.where(place >= starts[k], tiles[k], value)
            value = jnp.where(place < fill, value, 0.0)
            for c in range(9):
                staged[q * 9 + c] = jnp.broadcast_to(value[c : c + 1, :], (8, LANES))

        def chunk(n, size, start):
            tile = turned[pl.ds(start, size), :]
            mine = [
                [jnp.broadcast_to(tile[8 * h : 8 * h + 8, c : c + 1], (8, LANES)) for c in range(9)]
                for h in range(size // 8)
            ]
            total = [[None] * 3 for _ in range(size // 8)]
            for k in range(n):
                other = [staged[k * 9 + c] for c in range(9)]
                for h in range(size // 8):
                    me = mine[h]
                    d = [me[c] - other[c] for c in range(3)]
                    radius = d[0] * d[0] + d[1] * d[1] + d[2] * d[2] + SOFTEN_NEAR
                    inverse = lax.rsqrt(radius)
                    bb = me[3] * other[3] + me[4] * other[4] + me[5] * other[5]
                    ll = me[6] * other[6] + me[7] * other[7] + me[8] * other[8]
                    weight = (bb * ll) * (inverse * inverse * inverse)
                    for c in range(3):
                        term = weight * d[c]
                        total[h][c] = term if k == 0 else total[h][c] + term
            for h in range(size // 8):
                out = jnp.zeros((8, LANES), jnp.float32)
                for c in range(3):
                    out = jnp.where(
                        lane[0:8] == c, jnp.sum(total[h][c], axis=1, keepdims=True), out
                    )
                sums[pl.ds(start + 8 * h, 8), :] = out[:, 0:8]

        whole = lax.div(count + STEP - 1, 2 * STEP)
        odd = count > whole * 2 * STEP

        for n in range(1, 8):

            @pl.when(used == n)
            def _():
                def double(i, carry):
                    chunk(n, 2 * STEP, pl.multiple_of(i * 2 * STEP, 2 * STEP))
                    return carry

                lax.fori_loop(0, whole, double, 0)

                @pl.when(odd)
                def _():
                    chunk(n, STEP, pl.multiple_of(whole * 2 * STEP, 2 * STEP))

        flipped = sums[...].T
        alive = lane[0:1] < count
        for c in range(3):
            near[c, pl.ds(t, 1), :] = jnp.where(alive, flipped[c : c + 1, :], 0.0)
        return carry

    sums[...] = jnp.zeros_like(sums)
    lax.fori_loop(0, cells, near_cell, 0)

    mixed = jnp.dot(
        far[...], groups[...], precision=lax.Precision.HIGHEST, preferred_element_type=jnp.float32
    )
    burgers = [stacked[3 + c] for c in range(3)]
    line = [stacked[6 + c] for c in range(3)]
    pulled = []
    for r in range(3):
        value = 0.0
        for c in range(3):
            sigma = FAR_SCALE * mixed[:, 3 * r + c : 3 * r + c + 1] + stress[r, c]
            value = value + sigma * burgers[c]
        pulled.append(value)
    for c in range(3):
        a, b = (c + 1) % 3, (c + 2) % 3
        total = NEAR_SCALE * near[c] + (pulled[a] * line[b] - pulled[b] * line[a])
        near[c] = 0.5 * total

    node_rows = pos.shape[1]
    half = node_rows // 2
    acc[...] = jnp.zeros_like(acc)
    narrow = jnp.bfloat16
    high_ids = lax.broadcasted_iota(jnp.int32, (half, LANES), 0).astype(jnp.float32).astype(narrow)
    low_ids = lax.broadcasted_iota(jnp.int32, (LANES, LANES), 0).astype(jnp.float32).astype(narrow)
    groups_of = cells // 8
    zero = jnp.zeros((half, LANES), narrow)

    def tall(row, count):
        piece = jnp.broadcast_to(row, (16, LANES)).astype(narrow)
        return jnp.concatenate([piece] * (count // 16), axis=0)

    def scatter(step, carry):
        end, block = lax.div(step, groups_of), lax.rem(step, groups_of)
        start = pl.multiple_of(block * 8, 8)
        ids = connect[end, pl.ds(start, 8), :]
        values = [near[c, pl.ds(start, 8), :] for c in range(3)]
        parts = []
        for value in values:
            coarse = value.astype(narrow).astype(jnp.float32)
            parts += [coarse, value - coarse]
        node_row = lax.shift_right_logical(ids, 7)
        upper = node_row >= half
        hi = jnp.where(upper, node_row - half, node_row).astype(jnp.float32)
        lo = (ids & (LANES - 1)).astype(jnp.float32)
        low_half = jnp.where(upper, -1.0, lo)
        high_half = jnp.where(upper, lo, -1.0)
        one, none = jnp.ones((LANES, LANES), narrow), jnp.zeros((LANES, LANES), narrow)
        for k in range(8):
            span = slice(k * LANES, (k + 1) * LANES)
            mask = high_ids == tall(hi[k : k + 1, :], half)
            for m, part in enumerate(parts):
                left[m * half : (m + 1) * half, span] = jnp.where(
                    mask, tall(part[k : k + 1, :], half), zero
                )
            right[0:LANES, span] = jnp.where(
                low_ids == tall(low_half[k : k + 1, :], LANES), one, none
            )
            right[LANES : 2 * LANES, span] = jnp.where(
                low_ids == tall(high_half[k : k + 1, :], LANES), one, none
            )
        acc[...] += lax.dot_general(
            left[...], right[...], (((1,), (1,)), ((), ())), preferred_element_type=jnp.float32
        )
        return carry

    lax.fori_loop(0, 2 * groups_of, scatter, 0)
    edge = low.shape[1]
    for c in range(3):
        both = acc[2 * c * half : (2 * c + 1) * half, :] + acc[(2 * c + 1) * half : (2 * c + 2) * half, :]
        for s in range(2):
            span = slice(s * half, (s + 1) * half)
            velocity = both[:, s * LANES : (s + 1) * LANES] / drag[span, :]
            fields[3 + c, span, :] = velocity
            fields[c, span, :] = pos[c, span, :] + TIME_STEP * velocity
    for c in range(6):
        low[c] = fields[c, 0:edge, :]
        high[c] = fields[c, node_rows - edge : node_rows, :]


def edge_kernel(n, low, high, below, above, send, recv):
    me = lax.axis_index("gx")
    barrier = pltpu.get_barrier_semaphore()
    after, before = lax.rem(me + 1, n), lax.rem(me + n - 1, n)
    for peer in (after, before):
        pl.semaphore_signal(barrier, inc=1, device_id={"gx": peer}, device_id_type=MESH)
    pl.semaphore_wait(barrier, 2)

    def copy(slot, src, dst, peer):
        return pltpu.make_async_remote_copy(
            src_ref=src,
            dst_ref=dst,
            send_sem=send.at[slot],
            recv_sem=recv.at[slot],
            device_id={"gx": peer},
            device_id_type=MESH,
        )

    @pl.when(me < n - 1)
    def _():
        copy(0, high, below, after).start()

    @pl.when(me > 0)
    def _():
        copy(1, low, above, before).start()

    @pl.when(me < n - 1)
    def _():
        copy(0, high, below, after).wait_send()
        copy(1, low, above, before).wait_recv()

    @pl.when(me > 0)
    def _():
        copy(1, low, above, before).wait_send()
        copy(0, high, below, after).wait_recv()


def assemble_kernel(sizes, moves, fields, below, above, out, section):
    node_rows, edge, out_rows = fields.shape[1], below.shape[1], out.shape[1]
    nodes, margin = node_rows * LANES, edge * LANES
    section[:, 0:edge, :] = below[...]
    section[:, edge : edge + node_rows, :] = fields[...]
    section[:, edge + node_rows : 2 * edge + node_rows, :] = above[...]
    nx, ny, nz = sizes
    ix, iy, iz = [lax.axis_index(name) for name in AXES]
    at = lambda k, slab: moves[((k * nx + slab) * ny + iy) * nz + iz]
    up_own, down_own = at(0, ix), at(1, ix)
    up_prev = jnp.where(ix > 0, at(0, jnp.maximum(ix - 1, 0)), 0)
    down_next = jnp.where(ix < nx - 1, at(1, jnp.minimum(ix + 1, nx - 1)), 0)
    kept = nodes - up_own - down_own

    def shifted(c, by, first, count):
        row, turn = lax.div(by, LANES), lax.rem(by, LANES)
        lane = lax.broadcasted_iota(jnp.int32, (count, LANES), 1)
        back = lax.rem(LANES - turn, LANES)
        now = pltpu.roll(section[c, pl.ds(first + row, count), :], back, axis=1)
        later = pltpu.roll(section[c, pl.ds(first + row + 1, count), :], back, axis=1)
        return jnp.where(lane < LANES - turn, now, later)

    tail = out_rows - (4 * edge)
    position = (
        lax.broadcasted_iota(jnp.int32, (out_rows, LANES), 0) * LANES
        + lax.broadcasted_iota(jnp.int32, (out_rows, LANES), 1)
    )
    for c in range(6):
        out[c] = shifted(c, margin + down_own - up_prev, 0, out_rows)
        head = 2 * edge
        value = shifted(c, margin - up_prev, 0, head)
        out[c, 0:head, :] = jnp.where(position[0:head] < up_prev, value, out[c, 0:head, :])
        value = shifted(c, margin + nodes - up_prev - kept, tail, out_rows - tail)
        spot = position[tail:]
        value = jnp.where(spot < up_prev + kept, out[c, tail:out_rows, :], value)
        out[c, tail:out_rows, :] = jnp.where(spot < up_prev + kept + down_next, value, 0.0)


def shards(mesh, offsets, burgers, lines, counts, connect, node_pos, drag, stress, shifts):
    grid = offsets.shape[1:4]
    slots = offsets.shape[4]
    cells = grid[0] * grid[1] * grid[2]
    sizes = tuple(mesh.shape[name] for name in AXES)
    nx, ny, nz = sizes
    devices = nx * ny * nz
    half = [size // 2 for size in grid]
    local = half[0] * half[1] * half[2]
    nodes = node_pos.shape[4]
    node_rows, edge = nodes // LANES, MIG // LANES
    f32 = jnp.float32

    t = np.arange(cells)
    x, y, z = t // (grid[1] * grid[2]), t // grid[2] % grid[1], t % grid[2]
    coarse = ((x // 2) * half[1] + y // 2) * half[2] + z // 2
    lane = np.arange(LANES)
    code = np.where(lane[None, :] % local == coarse[:, None], lane[None, :] // local, -1)
    device = np.arange(devices)[:, None]
    inner = (lane % local)[None, :]
    centers = np.stack(
        [
            2 * (device // (ny * nz) * half[0] + inner // (half[1] * half[2])) + 1,
            2 * (device // nz % ny * half[1] + inner // half[2] % half[1]) + 1,
            2 * (device % nz * half[2] + inner % half[2]) + 1,
        ]
    ).astype(np.float32)
    groups = (lane[:, None] // local == lane[None, :]).astype(np.float32)

    flat = lambda array: array.reshape(array.shape[0], cells, slots)
    count_rows = counts.reshape(cells)
    face = (grid[1] * grid[2], grid[0] * grid[2], grid[0] * grid[1])
    face_shapes = [jax.ShapeDtypeStruct((2, 9, size, slots), f32) for size in face]

    stacked, fx, fy, fz, moments = pl.pallas_call(
        functools.partial(prep_kernel, grid),
        out_shape=[jax.ShapeDtypeStruct((9, cells, slots), f32)]
        + face_shapes
        + [jax.ShapeDtypeStruct((1, LANES), f32)],
        in_specs=[VM] * 5,
        out_specs=[VM] * 5,
        name="prep",
    )(
        flat(offsets), flat(burgers), flat(lines),
        jnp.broadcast_to(count_rows[:, None], (cells, LANES)), jnp.asarray(code, jnp.int32),
    )

    steps = sum(sizes) - 3
    hx, hy, hz, gathered = pl.pallas_call(
        functools.partial(exchange_kernel, sizes),
        out_shape=face_shapes + [jax.ShapeDtypeStruct((devices, 1, LANES), f32)],
        in_specs=[VM] * 4,
        out_specs=[VM] * 4,
        scratch_shapes=[
            pltpu.SemaphoreType.DMA((6,)),
            pltpu.SemaphoreType.DMA((6,)),
            pltpu.SemaphoreType.DMA((steps,)),
            pltpu.SemaphoreType.DMA((steps,)),
            pltpu.SemaphoreType.DMA,
        ],
        compiler_params=pltpu.CompilerParams(collective_id=0, has_side_effects=True),
        name="exchange",
    )(fx, fy, fz, moments.reshape(1, 1, LANES))

    edge_shape = jax.ShapeDtypeStruct((6, edge, LANES), f32)
    fields, low, high = pl.pallas_call(
        functools.partial(force_kernel, grid, sizes),
        out_shape=[jax.ShapeDtypeStruct((6, node_rows, LANES), f32), edge_shape, edge_shape],
        in_specs=[SM] * 2 + [VM] * 10,
        out_specs=[VM] * 3,
        scratch_shapes=[
            pltpu.VMEM(((cells + 2 * sum(face)) * ROWS, LANES), f32),
            pltpu.VMEM((63, 8, LANES), f32),
            pltpu.VMEM((LANES, ROWS), f32),
            pltpu.VMEM((LANES, 8), f32),
            pltpu.VMEM((3, cells, LANES), f32),
            pltpu.VMEM((cells, LANES), f32),
            pltpu.VMEM((3 * node_rows, 8 * LANES), jnp.bfloat16),
            pltpu.VMEM((2 * LANES, 8 * LANES), jnp.bfloat16),
            pltpu.VMEM((3 * node_rows, 2 * LANES), f32),
        ],
        name="forces",
    )(
        count_rows, stress,
        stacked, hx, hy, hz, gathered.reshape(devices, LANES),
        jnp.asarray(centers), jnp.asarray(groups),
        flat(connect), node_pos.reshape(3, node_rows, LANES), drag.reshape(node_rows, LANES),
    )

    below, above = pl.pallas_call(
        functools.partial(edge_kernel, nx),
        out_shape=[edge_shape, edge_shape],
        in_specs=[VM] * 2,
        out_specs=[VM] * 2,
        scratch_shapes=[pltpu.SemaphoreType.DMA((2,)), pltpu.SemaphoreType.DMA((2,))],
        compiler_params=pltpu.CompilerParams(collective_id=1, has_side_effects=True),
        name="edges",
    )(low, high)

    out_rows = node_rows + 2 * edge
    result = pl.pallas_call(
        functools.partial(assemble_kernel, sizes),
        out_shape=jax.ShapeDtypeStruct((6, out_rows, LANES), f32),
        in_specs=[SM] + [VM] * 3,
        out_specs=VM,
        scratch_shapes=[pltpu.VMEM((6, out_rows + 4 * edge, LANES), f32)],
        name="assemble",
    )(shifts.reshape(-1), fields, below, above)
    return result.reshape(6, 1, 1, 1, out_rows * LANES)


def solution(mesh):
    return jax.shard_map(
        functools.partial(shards, mesh),
        mesh=mesh,
        in_specs=(
            P(None, "gx", "gy", "gz", None),
            P(None, "gx", "gy", "gz", None),
            P(None, "gx", "gy", "gz", None),
            P("gx", "gy", "gz"),
            P(None, "gx", "gy", "gz", None),
            P(None, "gx", "gy", "gz", None),
            P("gx", "gy", "gz", None),
            P(),
            P(),
        ),
        out_specs=P(None, "gx", "gy", "gz", None),
        check_vma=False,
    )
```
